32 devices in a mesh: fsdp: 8 (over z, x), tp: 4 (over y, core).
Axes of the slice: x: 2, y: 2, z: 4, core: 2. Of those that a mesh axis runs over, the one named last changes fastest.
Arguments:
- tokens: bfloat16 [16, 256, 2048], P('fsdp', 'tp'), may hold values from -6 to 6
- cotangent: bfloat16 [16, 256, 2048], P('fsdp', 'tp'), may hold values from -6 to 6
- slot_order: int32 [16], replicated, may hold values from 0 to 15, each once
- seq_lengths: int32 [16], replicated, may hold values from 1 to 256, 2560 in all
- seq_offsets: int32 [16], replicated, may hold values from 0 to 4095
- attn_gain: bfloat16 [2048], P(('fsdp', 'tp')), may hold values from 0.5 to 1.5
- query_weight: bfloat16 [2048, 2048], P('fsdp', 'tp'), may hold values from -0.125 to 0.125
- query_down: bfloat16 [2048, 256], P(('fsdp', 'tp')), may hold values from -0.125 to 0.125
- query_up: bfloat16 [256, 2048], P('fsdp', 'tp'), may hold values from -0.375 to 0.375
- keyval_weight: bfloat16 [2, 2048, 256], P(None, ('fsdp', 'tp')), may hold values from -0.125 to 0.125
- keyval_down: bfloat16 [2, 2048, 256], P(None, ('fsdp', 'tp')), may hold values from -0.125 to 0.125
- keyval_up: bfloat16 [2, 256, 256], P(None, ('fsdp', 'tp')), may hold values from -0.375 to 0.375
- merge_weight: bfloat16 [2048, 2048], P('tp', 'fsdp'), may hold values from -0.25 to 0.25
- merge_down: bfloat16 [2048, 256], P('tp', 'fsdp'), may hold values from -0.25 to 0.25
- merge_up: bfloat16 [256, 2048], P(('fsdp', 'tp')), may hold values from -0.375 to 0.375
- ffn_gain: bfloat16 [2048], P(('fsdp', 'tp')), may hold values from 0.5 to 1.5
- expand_weight: bfloat16 [2, 2048, 16384], P(None, 'fsdp', 'tp'), may hold values from -0.125 to 0.125
- expand_down: bfloat16 [2, 2048, 256], P(None, ('fsdp', 'tp')), may hold values from -0.125 to 0.125
- expand_up: bfloat16 [2, 256, 16384], P(None, 'fsdp', 'tp'), may hold values from -0.375 to 0.375
- shrink_weight: bfloat16 [16384, 2048], P('tp', 'fsdp'), may hold values from -0.046875 to 0.046875
- shrink_down: bfloat16 [16384, 256], P('tp', 'fsdp'), may hold values from -0.046875 to 0.046875
- shrink_up: bfloat16 [256, 2048], P(('fsdp', 'tp')), may hold values from -0.375 to 0.375
Outputs:
- layer_out: bfloat16 [16, 256, 2048], P('fsdp', 'tp')
- input_grad: bfloat16 [16, 256, 2048], P('fsdp', 'tp')
- attngain_grad: float32 [2048], P(('fsdp', 'tp'))
- queryweight_grad: float32 [2048, 2048], P('fsdp', 'tp')
- querydown_grad: float32 [2048, 256], P(('fsdp', 'tp'))
- queryup_grad: float32 [256, 2048], P('fsdp', 'tp')
- keyvalweight_grad: float32 [2, 2048, 256], P(None, ('fsdp', 'tp'))
- keyvaldown_grad: float32 [2, 2048, 256], P(None, ('fsdp', 'tp'))
- keyvalup_grad: float32 [2, 256, 256], P(None, ('fsdp', 'tp'))
- mergeweight_grad: float32 [2048, 2048], P('tp', 'fsdp')
- mergedown_grad: float32 [2048, 256], P('tp', 'fsdp')
- mergeup_grad: float32 [256, 2048], P(('fsdp', 'tp'))
- ffngain_grad: float32 [2048], P(('fsdp', 'tp'))
- expandweight_grad: float32 [2, 2048, 16384], P(None, 'fsdp', 'tp')
- expanddown_grad: float32 [2, 2048, 256], P(None, ('fsdp', 'tp'))
- expandup_grad: float32 [2, 256, 16384], P(None, 'fsdp', 'tp')
- shrinkweight_grad: float32 [16384, 2048], P('tp', 'fsdp')
- shrinkdown_grad: float32 [16384, 256], P('tp', 'fsdp')
- shrinkup_grad: float32 [256, 2048], P(('fsdp', 'tp'))
The draws below stay inside these ranges and needn't reach their ends.
Inputs may be any that keep to these rules, and one draw needn't show every extreme that they name: `slot_order`: each of the 16 sequences is held by exactly one slot. `seq_lengths`: the lengths sum to 2560 and the longest is exactly 256.
All inputs are finite; a program needn't handle non-finite values.
Results may differ from the reference program's by a relative error of at most 0.028.
Values may be sent and summed in bfloat16 or wider, within the bound.
No kernel may reach another device: no remote copies, remote signals or barrier semaphores. Data moves between devices by JAX's collectives and lax.ppermute only.
A program may use at most 448 MiB of HBM per device.

```python
import math
import jax
import jax.numpy as jnp
import numpy as np
from jax import lax

D = 2048
H = 8
HD = 256
FF = 16384
R = 256
SPG = 2
LMAX = 256
NSEQ = 16
N_TP = 4


def touch_ends(values, rng, smallest, top_value):
    place = [jax.random.randint(jax.random.fold_in(rng, axis), (), 0, length) for axis, length in enumerate(values.shape)]
    longest = values.shape.index(max(values.shape))
    next_to = place[:longest] + [(place[longest] + 1) % values.shape[longest]] + place[longest + 1:]
    return values.at[tuple(place)].set(smallest).at[tuple(next_to)].set(top_value)


def shard_levels(stream_key, shape, split, least, top_value):
    factor_of = 1.0
    for dim, parts in split:
        steps = jax.random.uniform(jax.random.fold_in(jax.random.fold_in(stream_key, 6), dim), (parts,), jnp.float32, least / len(split), top_value / len(split))
        factor_of = factor_of * jnp.repeat(jnp.exp(steps), shape[dim] // parts).reshape((-1,) + (1,) * (len(shape) - 1 - dim))
    return factor_of


def profile(count, total, reach, lean):
    loads = [(1 << 20) // math.isqrt(rank ** lean) + 1 for rank in range(2, count + 1)]
    rest, given = total - reach - (count - 1), [1] * (count - 1)
    while rest > 0:
        candidates = [i for i in range(count - 1) if given[i] < reach]
        mass, remaining = sum([loads[i] for i in candidates]), rest
        for i in candidates:
            extra = min(reach - given[i], max(1, remaining * loads[i] // mass), rest)
            given[i] = given[i] + extra
            rest = rest - extra
    return np.array([reach] + given)


def ragged(own_key, amount, total, reach, slope):
    if amount == 2:
        one = jax.random.randint(own_key, (), max(1, total - reach), min(reach, total - 1) + 1)
        return jnp.stack([one, total - one])
    lengths = jnp.asarray(profile(amount, total, reach, slope), jnp.int32)
    pairs = (amount - 1) // 2
    giver, sink = lengths[1:1 + 2 * pairs:2], lengths[2:2 + 2 * pairs:2]
    margin = jnp.minimum(giver - 1, reach - sink)
    shifted = jax.random.randint(jax.random.fold_in(own_key, 1), (pairs,), 0, 1 << 20) % (margin + 1)
    lengths = lengths.at[1:1 + 2 * pairs:2].set(giver - shifted).at[2:2 + 2 * pairs:2].set(sink + shifted)
    return lengths[jax.random.permutation(jax.random.fold_in(own_key, 2), amount)]


def bell_draw(own_key, dims, scale, limit, cuts=(), kind=jnp.bfloat16):
    values = jax.random.normal(own_key, dims, jnp.float32) * scale
    if len(cuts) > 0:
        values = shard_levels(own_key, dims, cuts, -0.22, 0.18) * values
    return jnp.clip(values, min=-limit, max=limit).astype(kind)


def setup_inputs(seed: int = 0) -> dict:
    key_of = jax.random.split(jax.random.key(seed), 23)
    tokens = bell_draw(key_of[0], (NSEQ, LMAX, D), 1.0, 6.0, ((0, 8), (1, 4)))
    cotangent = bell_draw(key_of[1], (NSEQ, LMAX, D), 1.0, 6.0, ((0, 8), (1, 4)))
    slot_order = jax.random.permutation(key_of[2], NSEQ).astype(jnp.int32)
    seq_lengths = ragged(key_of[3], NSEQ, 5 * NSEQ * LMAX // 8, LMAX, 1).astype(jnp.int32)
    seq_offsets = touch_ends(jax.random.randint(key_of[4], (NSEQ,), 0, 4096), jax.random.fold_in(key_of[4], 1), 0, 4095).astype(jnp.int32)
    attn_gain = jnp.clip(1.0 + 0.1 * jax.random.normal(key_of[5], (D,), jnp.float32), 0.5, 1.5).astype(jnp.bfloat16)
    query_weight = bell_draw(key_of[6], (D, H * HD), D ** -0.5, 0.125, ((0, 8), (1, 4)))
    query_down = bell_draw(key_of[7], (D, R), D ** -0.5, 0.125, ((0, 32),))
    query_up = bell_draw(key_of[8], (R, H * HD), R ** -0.5, 0.375, ((0, 8), (1, 4)))
    keyval_weight = bell_draw(key_of[9], (2, D, HD), D ** -0.5, 0.125, ((1, 32),))
    keyval_down = bell_draw(key_of[10], (2, D, R), D ** -0.5, 0.125, ((1, 32),))
    keyval_up = bell_draw(key_of[11], (2, R, HD), R ** -0.5, 0.375, ((1, 32),))
    merge_weight = bell_draw(key_of[12], (H * HD, D), (H * HD // 4) ** -0.5, 0.25, ((0, 4), (1, 8)))
    merge_down = bell_draw(key_of[13], (H * HD, R), (H * HD // 4) ** -0.5, 0.25, ((0, 4), (1, 8)))
    merge_up = bell_draw(key_of[14], (R, D), R ** -0.5, 0.375, ((0, 32),))
    ffn_gain = jnp.clip(1.0 + 0.1 * jax.random.normal(key_of[15], (D,), jnp.float32), 0.5, 1.5).astype(jnp.bfloat16)
    expand_weight = bell_draw(key_of[16], (2, D, FF), D ** -0.5, 0.125, ((1, 8), (2, 4)))
    expand_down = bell_draw(key_of[17], (2, D, R), D ** -0.5, 0.125, ((1, 32),))
    expand_up = bell_draw(key_of[18], (2, R, FF), R ** -0.5, 0.375, ((1, 8), (2, 4)))
    shrink_weight = bell_draw(key_of[19], (FF, D), FF ** -0.5, 0.046875, ((0, 4), (1, 8)))
    shrink_down = bell_draw(key_of[20], (FF, R), FF ** -0.5, 0.046875, ((0, 4), (1, 8)))
    shrink_up = bell_draw(key_of[21], (R, D), R ** -0.5, 0.375, ((0, 32),))
    return dict(tokens=tokens, cotangent=cotangent, slot_order=slot_order, seq_lengths=seq_lengths, seq_offsets=seq_offsets, attn_gain=attn_gain, query_weight=query_weight, query_down=query_down, query_up=query_up, keyval_weight=keyval_weight, keyval_down=keyval_down, keyval_up=keyval_up, merge_weight=merge_weight, merge_down=merge_down, merge_up=merge_up, ffn_gain=ffn_gain, expand_weight=expand_weight, expand_down=expand_down, expand_up=expand_up, shrink_weight=shrink_weight, shrink_down=shrink_down, shrink_up=shrink_up)


@jax.custom_vjp
def low(v):
    return lax.optimization_barrier(v.astype(jnp.bfloat16)).astype(jnp.float32)

@jax.custom_vjp
def low_back(v):
    return v

def low_keep(v):
    return (low(v), None)

def low_pass(kept, grad):
    return (grad,)

def back_keep(v):
    return (v, None)

def back_low(kept, grad):
    return (low(grad),)
low.defvjp(low_keep, low_pass)
low_back.defvjp(back_keep, back_low)
HIGHEST = lax.Precision.HIGHEST

def matmul(left, right):
    return jnp.dot(left, right, precision=HIGHEST)

def norm_rows(values, gain):
    return values * lax.rsqrt(lax.optimization_barrier(jnp.mean(values * values, axis=-1, keepdims=True)) + 1e-06) * gain

def rotate(values, cosine, sine, turning):
    middle = values.shape[-1] // 2
    former = values[..., :middle]
    latter = values[..., middle:]
    return jnp.concatenate([former * cosine - turning * latter * sine, latter * cosine + turning * former * sine], axis=-1)

def rope_tables(positions):
    middle = HD // 2
    spread = jnp.power(10000.0, -2.0 * jnp.arange(middle, dtype=jnp.float32) / HD)
    angles = positions.astype(jnp.float32)[..., None] * spread
    return (jnp.cos(angles), jnp.sin(angles))

def pack_mask(slot_lengths):
    rows_all = jnp.arange(SPG * LMAX, dtype=jnp.int32)
    within = rows_all % LMAX
    limits = jnp.repeat(slot_lengths, LMAX)
    usable = within < limits
    return (rows_all[None, :] <= rows_all[:, None]) & usable[None, :]

def pack_forward(params, pack_tokens, slot_lengths, slot_offsets):
    attn_gain, query_weight, query_down, query_up, keyval_weight, keyval_down, keyval_up, merge_weight, merge_down, merge_up, ffn_gain, expand_weight, expand_down, expand_up, shrink_weight, shrink_down, shrink_up = params
    packed = SPG * LMAX
    tokens_flat = pack_tokens.reshape(packed, D)
    in_attn = low(norm_rows(tokens_flat, attn_gain))
    positions = slot_offsets[:, None] + jnp.arange(LMAX, dtype=jnp.int32)[None, :]
    cosine, sine = rope_tables(positions)
    cosine = cosine.reshape(packed, HD // 2)
    sine = sine.reshape(packed, HD // 2)
    allowed = pack_mask(slot_lengths)
    heads = H // N_TP
    group_width = heads * HD
    low_query = low(matmul(in_attn, query_down))
    low_key = low(matmul(in_attn, keyval_down[0]))
    low_value = low(matmul(in_attn, keyval_down[1]))
    attn_sum = jnp.zeros((packed, D), jnp.float32)
    for group in range(N_TP):
        first = group * group_width
        last = first + group_width
        query = low_back(matmul(in_attn, query_weight[:, first:last]) + matmul(low_back(low_query), query_up[:, first:last]))
        key = low_back(matmul(in_attn, keyval_weight[0]) + matmul(low_back(low_key), keyval_up[0]))
        value = low_back(low(matmul(in_attn, keyval_weight[1]) + matmul(low_back(low_value), keyval_up[1])))
        query_rot = low(rotate(query.reshape(packed, heads, HD), cosine[:, None, :], sine[:, None, :], 1.0))
        key_rot = low(rotate(key, cosine, sine, 1.0))
        scores = low_back(jnp.einsum('phd,kd->hpk', query_rot, key_rot, precision=HIGHEST) * HD ** (-0.5))
        scores = jnp.where(allowed[None], scores, -1e+30)
        highest = lax.optimization_barrier(jnp.max(scores, axis=-1, keepdims=True))
        expo = jnp.exp(scores - highest)
        probs = expo / lax.optimization_barrier(jnp.sum(expo, axis=-1, keepdims=True))
        mixed = low_back(low(jnp.einsum('hpk,kd->phd', low(probs), value, precision=HIGHEST))).reshape(packed, group_width)
        merged = low_back(low(matmul(mixed, merge_down[first:last])))
        attn_sum = attn_sum + matmul(mixed, merge_weight[first:last]) + matmul(merged, merge_up)
    middle = tokens_flat + low_back(attn_sum)
    feedforward_input = low(norm_rows(middle, ffn_gain))
    gate_lowrank = low(matmul(feedforward_input, expand_down[0]))
    up_lowrank = low(matmul(feedforward_input, expand_down[1]))
    ffn_width = FF // N_TP
    ffn_sum = jnp.zeros((packed, D), jnp.float32)
    for group in range(N_TP):
        first = group * ffn_width
        last = first + ffn_width
        gate_value = low_back(matmul(feedforward_input, expand_weight[0][:, first:last]) + matmul(low_back(gate_lowrank), expand_up[0][:, first:last]))
        upward_value = low_back(matmul(feedforward_input, expand_weight[1][:, first:last]) + matmul(low_back(up_lowrank), expand_up[1][:, first:last]))
        hidden = low_back(low(jax.nn.gelu(gate_value, approximate=True) * upward_value))
        shrunk = low_back(low(matmul(hidden, shrink_down[first:last])))
        ffn_sum = ffn_sum + matmul(hidden, shrink_weight[first:last]) + matmul(shrunk, shrink_up)
    return (middle + low_back(ffn_sum)).reshape(SPG, LMAX, D)

def reference(tokens, cotangent, slot_order, seq_lengths, seq_offsets, attn_gain, query_weight, query_down, query_up, keyval_weight, keyval_down, keyval_up, merge_weight, merge_down, merge_up, ffn_gain, expand_weight, expand_down, expand_up, shrink_weight, shrink_down, shrink_up):
    params = tuple((array_item.astype(jnp.float32) for array_item in (attn_gain, query_weight, query_down, query_up, keyval_weight, keyval_down, keyval_up, merge_weight, merge_down, merge_up, ffn_gain, expand_weight, expand_down, expand_up, shrink_weight, shrink_down, shrink_up)))
    groups = NSEQ // SPG
    row_ids = jnp.arange(LMAX, dtype=jnp.int32)
    valid = (row_ids[None, :] < seq_lengths[:, None]).astype(jnp.float32)
    slot_tokens = tokens.astype(jnp.float32)[slot_order]
    slot_cot = (cotangent.astype(jnp.float32) * valid[..., None])[slot_order]
    slot_lengths = seq_lengths[slot_order].reshape(groups, SPG)
    slot_offsets = seq_offsets[slot_order].reshape(groups, SPG)

    def whole(slot_values, *weights):
        step = jax.checkpoint(lambda item: pack_forward(weights, item[0], item[1], item[2]))
        result = lax.map(step, (slot_values.reshape(groups, SPG, LMAX, D), slot_lengths, slot_offsets))
        return result.reshape(NSEQ, LMAX, D)
    layer, pull = jax.vjp(whole, slot_tokens, *params)
    grads = pull(slot_cot)
    inverse = jnp.zeros((NSEQ,), jnp.int32).at[slot_order].set(jnp.arange(NSEQ, dtype=jnp.int32))
    return (layer[inverse].astype(jnp.bfloat16), grads[0][inverse].astype(jnp.bfloat16), grads[1], grads[2], grads[3], grads[4], grads[5], grads[6], grads[7], grads[8], grads[9], grads[10], grads[11], grads[12], grads[13], grads[14], grads[15], grads[16], grads[17])
```

```python
import jax
import jax.numpy as jnp
from jax import lax
from jax.experimental import pallas as pl
from jax.experimental.pallas import tpu as pltpu
from jax.sharding import PartitionSpec as P

HD = 256
SPG = 2
LMAX = 256
EPSILON = 1e-06
BF = jnp.bfloat16
F32 = jnp.float32
BOTH = ("fsdp", "tp")


def mm(form, left, right):
    return jnp.einsum(form, left, right, preferred_element_type=F32)


def norm_rows(values, gain):
    return values * lax.rsqrt(jnp.mean(values * values, axis=-1, keepdims=True) + EPSILON) * gain


def rotate(values, cosine, sine, turning):
    middle = values.shape[-1] // 2
    former = values[..., :middle]
    latter = values[..., middle:]
    return jnp.concatenate(
        [former * cosine - turning * latter * sine, latter * cosine + turning * former * sine],
        axis=-1,
    )


def rope_tables(positions):
    middle = HD // 2
    spread = jnp.power(10000.0, -2.0 * jnp.arange(middle, dtype=F32) / HD)
    angles = positions.astype(F32)[..., None] * spread
    return (jnp.cos(angles), jnp.sin(angles))


def deal_kernel(index_ref, limit_ref, source_ref, out_ref):
    block = pl.program_id(0)
    rows = lax.broadcasted_iota(jnp.int32, source_ref.shape, 1)
    values = source_ref[...]
    out_ref[...] = jnp.where(rows < limit_ref[block], values, jnp.zeros_like(values))


def deal_blocks(values, index, limits):
    count, rows, width = values.shape
    return pl.pallas_call(
        deal_kernel,
        grid_spec=pltpu.PrefetchScalarGridSpec(
            num_scalar_prefetch=2,
            grid=(count,),
            in_specs=[pl.BlockSpec((1, rows, width), lambda b, index, limits: (index[b], 0, 0))],
            out_specs=pl.BlockSpec((1, rows, width), lambda b, index, limits: (b, 0, 0)),
        ),
        out_shape=jax.ShapeDtypeStruct(values.shape, values.dtype),
    )(index, limits, values)


def gather_all(values):
    return lax.all_gather(values, BOTH, axis=0, tiled=True)


def gather_fsdp(values):
    return lax.all_gather(values, "fsdp", axis=0, tiled=True)


def gather_rows(values):
    return lax.all_gather(values, "tp", axis=0, tiled=True)


def scatter_all(values):
    return lax.psum_scatter(values.astype(BF), BOTH, scatter_dimension=0, tiled=True)


def scatter_fsdp(values):
    return lax.psum_scatter(values.astype(BF), "fsdp", scatter_dimension=0, tiled=True)


def sum_rows(values):
    return lax.psum_scatter(values.astype(BF), "tp", scatter_dimension=0, tiled=True).astype(F32)


def exchange(values):
    return lax.all_to_all(values, "fsdp", 0, 0, tiled=False)


def cut(values, sizes):
    pieces = []
    start = 0
    for size in sizes:
        pieces.append(values[:, start : start + size])
        start += size
    return pieces


def spread(values, parts):
    two, rows, cols = values.shape
    return (
        values.reshape(two, parts, rows // parts, cols)
        .transpose(1, 0, 2, 3)
        .reshape(parts, two * (rows // parts), cols)
    )


def unspread(values, two):
    parts, rows, cols = values.shape
    return (
        values.reshape(parts, two, rows // two, cols)
        .transpose(1, 0, 2, 3)
        .reshape(two, parts * (rows // two), cols)
    )


def wide_to_rows(values, parts):
    return values.reshape(parts, values.shape[0] // parts * (values.shape[1] // HD), HD)


def per_device(
    tokens,
    cotangent,
    slot_order,
    seq_lengths,
    seq_offsets,
    attn_gain,
    query_weight,
    query_down,
    query_up,
    keyval_weight,
    keyval_down,
    keyval_up,
    merge_weight,
    merge_down,
    merge_up,
    ffn_gain,
    expand_weight,
    expand_down,
    expand_up,
    shrink_weight,
    shrink_down,
    shrink_up,
):

    nf = lax.axis_size("fsdp")
    nt = lax.axis_size("tp")
    nd = nf * nt
    fsdp_index = lax.axis_index("fsdp")
    tp_index = lax.axis_index("tp")
    quarter = tokens.shape[1]
    width = tokens.shape[2]
    packed = SPG * LMAX
    own = SPG * quarter
    scale = HD ** (-0.5)
    seq_count = slot_order.shape[0]
    cols = query_weight.shape[1]
    heads = cols // HD
    ds = query_weight.shape[0]
    rs = query_up.shape[0]
    rank = rs * nf
    d1 = query_down.shape[0]
    r1 = merge_up.shape[0]
    units = expand_weight.shape[2]
    fs = units // nf
    wide = width // HD

    mine = lax.dynamic_slice_in_dim(slot_order, fsdp_index * SPG, SPG)
    slot_lengths = jnp.take(seq_lengths, mine)
    slot_offsets = jnp.take(seq_offsets, mine)
    slot_ids = jnp.arange(seq_count, dtype=jnp.int32)
    homes = jnp.sum(
        jnp.where(slot_order[None, :] == slot_ids[:, None], slot_ids[None, :], 0), axis=1
    )
    blocks = jnp.arange(nd * SPG, dtype=jnp.int32)
    block_slot = (blocks // (nt * SPG)) * SPG + blocks % SPG
    block_part = (blocks // SPG) % nt

    def block_of(slot):
        return (slot // SPG) * (nt * SPG) + block_part * SPG + slot % SPG

    to_slots = block_of(jnp.take(slot_order, block_slot))
    to_given = block_of(jnp.take(homes, block_slot))
    slot_limits = jnp.take(seq_lengths, jnp.take(slot_order, block_slot)) - block_part * quarter
    whole_limits = jnp.full((nd * SPG,), quarter, jnp.int32)

    tokens_all = gather_fsdp(tokens)
    x_here = jnp.concatenate(
        [
            lax.dynamic_index_in_dim(tokens_all, mine[slot], 0, keepdims=False)
            for slot in range(SPG)
        ],
        axis=0,
    ).astype(F32)
    gains = jnp.pad(
        jnp.concatenate([attn_gain, ffn_gain]).reshape(1, 2 * d1), ((0, 15), (0, HD - 2 * d1))
    )
    factor_sizes = (d1, 2 * d1, 2 * d1, 2 * d1, 2 * r1, r1 * wide, r1 * wide, 16)
    factors = gather_all(
        jnp.concatenate(
            [
                query_down,
                keyval_weight.reshape(2 * d1, HD),
                keyval_down.reshape(2 * d1, rank),
                expand_down.reshape(2 * d1, rank),
                keyval_up.reshape(2 * r1, HD),
                merge_up.reshape(r1 * wide, HD),
                shrink_up.reshape(r1 * wide, HD),
                gains,
            ],
            axis=0,
        )
    ).reshape(nd, sum(factor_sizes), HD)
    qdown, kvw, kvd, edown, kvu, mup, sup, gains = cut(factors, factor_sizes)
    qdown = qdown.reshape(width, rank)
    kvw = unspread(kvw, 2)
    kvd = unspread(kvd, 2)
    edown = unspread(edown, 2)
    kvu = unspread(kvu, 2)
    mup = mup.reshape(rank, width)
    sup = sup.reshape(rank, width)
    gain_one = gains[:, 0, :d1].reshape(width).astype(F32)
    gain_two = gains[:, 0, d1 : 2 * d1].reshape(width).astype(F32)
    proj_sizes = (ds, rs, ds, rs)
    projections = gather_fsdp(
        jnp.concatenate(
            [query_weight, query_up, merge_weight.reshape(ds, cols), merge_down.T], axis=0
        )
    ).reshape(nf, sum(proj_sizes), cols)
    wq, qup, wm, mdown = cut(projections, proj_sizes)
    wq = wq.reshape(width, cols)
    qup = qup.reshape(rank, cols)
    wm = wm.reshape(nf, cols, ds).transpose(1, 0, 2).reshape(cols, width)
    mdown = mdown.reshape(rank, cols)
    wq_full = (wq + mm("dr,re->de", qdown, qup)).astype(BF)
    wkv_full = (kvw + mm("idr,ire->ide", kvd, kvu)).astype(BF)
    wm_full = (wm + mm("re,rd->ed", mdown, mup)).astype(BF)

    first = jnp.concatenate(
        [expand_weight.reshape(2 * ds, units), expand_up.reshape(2 * rs, units), shrink_down.T],
        axis=0,
    )
    first = first.reshape(first.shape[0], nf, fs).transpose(1, 0, 2)
    first = exchange(first)
    second = exchange(shrink_weight.reshape(nf, fs, ds))
    ew, eup, sdown = cut(first, (2 * ds, 2 * rs, rs))
    ew = unspread(ew, 2)
    eup = unspread(eup, 2)
    sdown = sdown.reshape(rank, fs)
    sw = second.transpose(1, 0, 2).reshape(fs, width)
    ew_full = (ew + mm("idr,irf->idf", edown, eup)).astype(BF)
    sw_full = (sw + mm("rf,rd->fd", sdown, sup)).astype(BF)

    grad_ffn = deal_blocks(
        gather_all(cotangent.reshape(own, width)).reshape(nd * SPG, quarter, width),
        to_slots,
        slot_limits,
    ).reshape(nd * own, width)
    grad_out = lax.dynamic_slice_in_dim(
        grad_ffn, (fsdp_index * nt + tp_index) * own, own
    ).astype(F32)

    in_attn = gather_rows(norm_rows(x_here, gain_one).astype(BF))
    query = mm("pd,de->pe", in_attn, wq_full)
    key_raw = mm("pd,de->pe", in_attn, wkv_full[0])
    value_low = mm("pd,de->pe", in_attn, wkv_full[1]).astype(BF)
    rows_all = jnp.arange(packed, dtype=jnp.int32)
    row_slot = (rows_all // quarter) % SPG
    row_within = (rows_all // own) * quarter + rows_all % quarter
    row_place = row_slot * LMAX + row_within
    positions = jnp.where(row_slot == 0, slot_offsets[0], slot_offsets[1]) + row_within
    cosine, sine = rope_tables(positions)
    query_rot = rotate(
        query.reshape(packed, heads, HD), cosine[:, None, :], sine[:, None, :], 1.0
    ).astype(BF)
    key_rot = rotate(key_raw, cosine, sine, 1.0).astype(BF)
    usable = row_within < jnp.where(row_slot == 0, slot_lengths[0], slot_lengths[1])
    allowed = (row_place[None, :] <= row_place[:, None]) & usable[None, :]
    scores = jnp.where(allowed[None], mm("phd,kd->hpk", query_rot, key_rot) * scale, -1e30)
    highest = jnp.max(scores, axis=-1, keepdims=True)
    logsum = highest + jnp.log(jnp.sum(jnp.exp(scores - highest), axis=-1, keepdims=True))
    probs = jnp.exp(scores - logsum)
    probs_low = probs.astype(BF)
    mixed = mm("hpk,kd->phd", probs_low, value_low).astype(BF).reshape(packed, cols)
    x_mid = x_here + sum_rows(mm("pe,ed->pd", mixed, wm_full))

    in_ffn = gather_all(norm_rows(x_mid, gain_two).astype(BF))
    gate_value = mm("pd,df->pf", in_ffn, ew_full[0])
    upward_value = mm("pd,df->pf", in_ffn, ew_full[1])
    hidden = (jax.nn.gelu(gate_value, approximate=True) * upward_value).astype(BF)
    grad_hidden = mm("pd,fd->pf", grad_ffn, sw_full)

    def activate(gate_in, up_in):
        return jax.nn.gelu(gate_in, approximate=True) * up_in

    gate_grad, upward_grad = jax.vjp(activate, gate_value, upward_value)[1](grad_hidden)
    gate_grad = gate_grad.astype(BF)
    upward_grad = upward_grad.astype(BF)
    grad_in_ffn = scatter_all(
        mm("pf,df->pd", gate_grad, ew_full[0]) + mm("pf,df->pd", upward_grad, ew_full[1])
    ).astype(F32)
    shrink_grad = mm("pf,pd->fd", hidden, grad_ffn).astype(BF)
    expand_grad = jnp.stack(
        [
            mm("pd,pf->df", in_ffn, gate_grad).astype(BF),
            mm("pd,pf->df", in_ffn, upward_grad).astype(BF),
        ]
    )
    sup_grad = mm("rf,fd->rd", sdown, shrink_grad)
    sdown_grad = mm("rd,fd->rf", sup, shrink_grad)
    eup_grad = mm("idr,idf->irf", edown, expand_grad)
    edown_grad = mm("idf,irf->idr", expand_grad, eup)
    first_grad = exchange(
        jnp.concatenate(
            [
                spread(expand_grad, nf),
                spread(eup_grad.astype(BF), nf),
                sdown_grad.astype(BF).reshape(nf, rs, fs),
            ],
            axis=1,
        )
    )
    second_grad = exchange(shrink_grad.reshape(fs, nf, ds).transpose(1, 0, 2))

    layer_part = mm(
        "pf,fd->pd",
        deal_blocks(
            hidden.reshape(nd * SPG, quarter, fs), to_given, whole_limits
        ).reshape(nd * own, fs),
        sw_full,
    ).astype(BF)
    for slot in range(SPG):
        start = (
            (mine[slot] // SPG) * (nt * SPG) + tp_index * SPG + mine[slot] % SPG
        ) * quarter
        kept = lax.dynamic_slice_in_dim(layer_part, start, quarter)
        kept = (kept.astype(F32) + x_mid[slot * quarter : (slot + 1) * quarter]).astype(BF)
        layer_part = lax.dynamic_update_slice_in_dim(layer_part, kept, start, 0)
    layer_out = scatter_all(layer_part).reshape(SPG, quarter, width)

    pull_two = jax.vjp(norm_rows, x_mid, gain_two)[1]
    grad_mid_part, ffngain_part = pull_two(grad_in_ffn)
    grad_mid = grad_out + grad_mid_part
    grad_attn = gather_rows(grad_mid.astype(BF))
    merge_grad = mm("pe,pd->ed", mixed, grad_attn).astype(BF)
    mup_grad = mm("re,ed->rd", mdown, merge_grad)
    mdown_grad = mm("rd,ed->re", mup, merge_grad)
    grad_mixed = mm("pd,ed->pe", grad_attn, wm_full).astype(BF).reshape(packed, heads, HD)
    grad_probs = mm("phd,kd->hpk", grad_mixed, value_low)
    grad_value = mm("hpk,phd->kd", probs_low, grad_mixed).astype(BF)
    inner = jnp.sum(grad_probs * probs, axis=-1, keepdims=True)
    grad_scores = (probs * (grad_probs - inner)).astype(BF)
    grad_qrot = mm("hpk,kd->phd", grad_scores, key_rot) * scale
    grad_krot = mm("hpk,phd->kd", grad_scores, query_rot) * scale
    grad_query = (
        rotate(grad_qrot, cosine[:, None, :], sine[:, None, :], -1.0)
        .reshape(packed, cols)
        .astype(BF)
    )
    grad_key = rotate(grad_krot, cosine, sine, -1.0).astype(BF)
    grad_in_attn = sum_rows(
        mm("pe,de->pd", grad_query, wq_full)
        + mm("pe,de->pd", grad_key, wkv_full[0])
        + mm("pe,de->pd", grad_value, wkv_full[1])
    )
    query_grad = mm("pd,pe->de", in_attn, grad_query).astype(BF)
    qup_grad = mm("dr,de->re", qdown, query_grad)
    qdown_grad = mm("de,re->dr", query_grad, qup)
    keyval_grad = jnp.stack(
        [
            mm("pd,pe->de", in_attn, grad_key).astype(BF),
            mm("pd,pe->de", in_attn, grad_value).astype(BF),
        ]
    )
    kvup_grad = mm("idr,ide->ire", kvd, keyval_grad)
    pull_one = jax.vjp(norm_rows, x_here, gain_one)[1]
    grad_x_part, attngain_part = pull_one(grad_in_attn)
    input_low = (grad_mid + grad_x_part).astype(BF).reshape(SPG, quarter, width)
    input_all = gather_fsdp(input_low)
    input_grad = jnp.concatenate(
        [
            lax.dynamic_slice_in_dim(
                input_all, jnp.take(homes, fsdp_index * SPG + slot), 1
            )
            for slot in range(SPG)
        ],
        axis=0,
    )

    proj_grads = scatter_fsdp(
        jnp.concatenate(
            [
                query_grad.reshape(nf, ds, cols),
                qup_grad.astype(BF).reshape(nf, rs, cols),
                merge_grad.reshape(cols, nf, ds).transpose(1, 0, 2).reshape(nf, ds, cols),
                mdown_grad.astype(BF).reshape(nf, rs, cols),
            ],
            axis=1,
        ).reshape(nf * sum(proj_sizes), cols)
    ).astype(F32)
    queryweight_grad = proj_grads[:ds]
    queryup_grad = proj_grads[ds : ds + rs]
    mergeweight_grad = proj_grads[ds + rs : 2 * ds + rs].reshape(cols, ds)
    mergedown_grad = proj_grads[2 * ds + rs :].T
    gain_parts = jnp.pad(
        jnp.concatenate(
            [attngain_part.reshape(nd, 1, d1), ffngain_part.reshape(nd, 1, d1)], axis=2
        ),
        ((0, 0), (0, 15), (0, HD - 2 * d1)),
    )
    sizes = (d1, 2 * d1, 2 * d1, 2 * r1, r1 * wide, r1 * wide, 16)
    factor_grads = scatter_all(
        jnp.concatenate(
            [
                qdown_grad.astype(BF).reshape(nd, d1, rank),
                spread(keyval_grad, nd),
                spread(edown_grad.astype(BF), nd),
                spread(kvup_grad.astype(BF), nd),
                wide_to_rows(mup_grad.astype(BF), nd),
                wide_to_rows(sup_grad.astype(BF), nd),
                gain_parts.astype(BF),
            ],
            axis=1,
        ).reshape(nd * sum(sizes), HD)
    ).astype(F32)[None]
    querydown_grad, kvw_grad, edn_grad, kvu_grad, mergeup_grad, shrinkup_grad, gain_grads = [
        piece[0] for piece in cut(factor_grads, sizes)
    ]
    keyvalweight_grad = kvw_grad.reshape(2, d1, HD)
    keyvaldown_grad = mm("ide,ire->idr", keyvalweight_grad.astype(BF), kvu)
    expanddown_grad = edn_grad.reshape(2, d1, rank)
    keyvalup_grad = kvu_grad.reshape(2, r1, HD)
    mergeup_grad = mergeup_grad.reshape(r1, width)
    shrinkup_grad = shrinkup_grad.reshape(r1, width)
    attngain_grad = gain_grads[0, :d1]
    ffngain_grad = gain_grads[0, d1 : 2 * d1]
    first_grad = (
        first_grad.transpose(1, 0, 2).reshape(first_grad.shape[1], units).astype(F32)
    )
    expandweight_grad = first_grad[: 2 * ds].reshape(2, ds, units)
    expandup_grad = first_grad[2 * ds : 2 * (ds + rs)].reshape(2, rs, units)
    shrinkdown_grad = first_grad[2 * (ds + rs) :].T
    shrinkweight_grad = second_grad.reshape(units, ds).astype(F32)
    return (
        layer_out,
        input_grad,
        attngain_grad,
        queryweight_grad,
        querydown_grad,
        queryup_grad,
        keyvalweight_grad,
        keyvaldown_grad,
        keyvalup_grad,
        mergeweight_grad,
        mergedown_grad,
        mergeup_grad,
        ffngain_grad,
        expandweight_grad,
        expanddown_grad,
        expandup_grad,
        shrinkweight_grad,
        shrinkdown_grad,
        shrinkup_grad,
    )


def solution(mesh):
    placed = (
        P("fsdp", "tp", None),
        P("fsdp", "tp", None),
        P(),
        P(),
        P(),
        P(("fsdp", "tp")),
        P("fsdp", "tp"),
        P(("fsdp", "tp"), None),
        P("fsdp", "tp"),
        P(None, ("fsdp", "tp"), None),
        P(None, ("fsdp", "tp"), None),
        P(None, ("fsdp", "tp"), None),
        P("tp", "fsdp"),
        P("tp", "fsdp"),
        P(("fsdp", "tp"), None),
        P(("fsdp", "tp")),
        P(None, "fsdp", "tp"),
        P(None, ("fsdp", "tp"), None),
        P(None, "fsdp", "tp"),
        P("tp", "fsdp"),
        P("tp", "fsdp"),
        P(("fsdp", "tp"), None),
    )
    return jax.shard_map(
        per_device,
        mesh=mesh,
        in_specs=placed,
        out_specs=(
            P("fsdp", "tp", None),
            P("fsdp", "tp", None),
            P(("fsdp", "tp")),
            P("fsdp", "tp"),
            P(("fsdp", "tp"), None),
            P("fsdp", "tp"),
            P(None, ("fsdp", "tp"), None),
            P(None, ("fsdp", "tp"), None),
            P(None, ("fsdp", "tp"), None),
            P("tp", "fsdp"),
            P("tp", "fsdp"),
            P(("fsdp", "tp"), None),
            P(("fsdp", "tp")),
            P(None, "fsdp", "tp"),
            P(None, ("fsdp", "tp"), None),
            P(None, "fsdp", "tp"),
            P("tp", "fsdp"),
            P("tp", "fsdp"),
            P(("fsdp", "tp"), None),
        ),
        check_vma=False,
    )
```
